32 devices in a mesh: freq: 8 (over z, x), unk: 4 (over y, core).
Axes of the slice: x: 2, y: 2, z: 4, core: 2. Of those that a mesh axis runs over, the one named last changes fastest.
Arguments:
- time_samples: bfloat16 [16, 32, 2048], P(None, 'freq', 'unk'), may hold values from -3 to 3
- inverse_offset: bfloat16 [2, 8, 2048, 512], P(None, 'freq', 'unk'), may hold values from -0.09375 to 0.09375
- coupling_near: bfloat16 [2, 8, 2048, 512], P(None, 'freq', 'unk'), may hold values from -0.125 to 0.125
- coupling_far: bfloat16 [2, 8, 2048, 512], P(None, 'freq', 'unk'), may hold values from -0.09375 to 0.09375
Outputs:
- solution: bfloat16 [2, 8, 32, 2048], P(None, 'freq', None, 'unk')
The draws below stay inside these ranges and needn't reach their ends.
All inputs are finite; a program needn't handle non-finite values.
Results may differ from the reference program's by a relative error of at most 0.017.
Values may be sent and summed in bfloat16 or wider, within the bound.
A program may use at most 64 MiB of HBM per device.

```python
import math
import jax
import jax.numpy as jnp
from jax import lax

ROWS = 512
FREQS = 8
TIMES = 16
LOADS = 32
UNKNOWNS = 2048


def shard_levels(stream_key, dims, cuts, low, top_value):
    def one(axis_at, parts):
        draws = jax.random.uniform(jax.random.fold_in(jax.random.fold_in(stream_key, 6), axis_at), (parts,), jnp.float32, low / len(cuts), top_value / len(cuts))
        return jnp.repeat(jnp.exp(draws), dims[axis_at] // parts).reshape((-1,) + (1,) * (len(dims) - axis_at - 1))

    level = one(*cuts[0])
    for cut in cuts[1:]:
        level = level * one(*cut)
    return level


def normal_values(stream_key, extent, width, bound, pieces=(), kind=jnp.bfloat16):
    values = width * jax.random.normal(stream_key, extent, jnp.float32)
    if pieces:
        values = values * shard_levels(stream_key, extent, pieces, -0.22, 0.18)
    return jnp.clip(values, -bound, bound).astype(kind)


def setup_inputs(seed: int = 0) -> dict:
    seeds = jax.random.split(jax.random.key(seed), 5)
    time_samples = normal_values(seeds[0], (TIMES, LOADS, UNKNOWNS), 0.5, 3.0, ((1, 8), (2, 4)))
    inverse_offset = normal_values(seeds[1], (2, FREQS, UNKNOWNS, ROWS), (ROWS * 8) ** -0.5, 0.09375, ((1, 8), (2, 4)))
    coupling_near = normal_values(seeds[2], (2, FREQS, UNKNOWNS, ROWS), (ROWS * 4) ** -0.5, 0.125, ((1, 8), (2, 4)))
    coupling_far = normal_values(seeds[3], (2, FREQS, UNKNOWNS, ROWS), (ROWS * 8) ** -0.5, 0.09375, ((1, 8), (2, 4)))
    return {"time_samples": time_samples, "inverse_offset": inverse_offset, "coupling_near": coupling_near, "coupling_far": coupling_far}


def complex_product(factor_one, factor_two):
    first_real = factor_one[0].astype(jnp.float32)
    first_imag = factor_one[1].astype(jnp.float32)
    second_real = factor_two[0].astype(jnp.float32)
    second_imag = factor_two[1].astype(jnp.float32)
    highest = lax.Precision.HIGHEST
    real_part = jnp.einsum('fmk,fkn->fmn', first_real, second_real, precision=highest) - jnp.einsum('fmk,fkn->fmn', first_imag, second_imag, precision=highest)
    imag_part = jnp.einsum('fmk,fkn->fmn', first_real, second_imag, precision=highest) + jnp.einsum('fmk,fkn->fmn', first_imag, second_real, precision=highest)
    return jnp.stack([real_part, imag_part])

def transform_table(time_count, freq_count):
    moment = jnp.arange(time_count, dtype=jnp.int32)
    harmonic = jnp.arange(freq_count, dtype=jnp.int32)
    phase_angle = (harmonic[:, None] * moment[None, :] % time_count).astype(jnp.float32) * (2.0 * math.pi / time_count)
    damping = jnp.power(0.5, moment.astype(jnp.float32) / time_count) / math.sqrt(time_count)
    return jnp.stack([damping * jnp.cos(phase_angle), -damping * jnp.sin(phase_angle)])

def reference(time_samples, inverse_offset, coupling_near, coupling_far):
    weights_table = transform_table(TIMES, FREQS)
    spectra = jnp.einsum('ckt,tln->ckln', weights_table, time_samples.astype(jnp.float32), precision=lax.Precision.HIGHEST).astype(jnp.bfloat16)
    blank_block = jnp.zeros((2, FREQS, LOADS, ROWS), jnp.bfloat16)
    previous = blank_block
    before_previous = blank_block
    solved = []
    for block_index in range(UNKNOWNS // ROWS):
        rows_slice = slice(block_index * ROWS, (block_index + 1) * ROWS)
        offset_block = inverse_offset[:, :, rows_slice, :]
        near_block = coupling_near[:, :, rows_slice, :]
        far_block = coupling_far[:, :, rows_slice, :]
        near_reduced = (near_block.astype(jnp.float32) + complex_product(near_block, offset_block)).astype(jnp.bfloat16)
        far_reduced = (far_block.astype(jnp.float32) + complex_product(far_block, offset_block)).astype(jnp.bfloat16)
        spectra_block = spectra[:, :, :, rows_slice]
        driven = spectra_block.astype(jnp.float32) + complex_product(spectra_block, offset_block)
        fresh_block = (driven - complex_product(previous, near_reduced) - complex_product(before_previous, far_reduced)).astype(jnp.bfloat16)
        solved.append(fresh_block)
        before_previous = previous
        previous = fresh_block
    return jnp.concatenate(solved, axis=3)
```

```python
import functools
import math

import jax
import jax.numpy as jnp
import numpy as np
from jax import lax
from jax.experimental import pallas as pl
from jax.experimental.pallas import tpu as pltpu
from jax.sharding import PartitionSpec as P

MESH = pl.DeviceIdType.MESH


def transform_matrix(times, freqs, loads):
    moment = np.arange(times)
    angle = (np.arange(freqs)[:, None] * moment[None, :] % times) * (2.0 * math.pi / times)
    damping = np.power(0.5, moment / times) / math.sqrt(times)
    table = np.stack([damping * np.cos(angle), -damping * np.sin(angle)], axis=1)
    full = np.einsum("kct,lm->kcltm", table, np.eye(loads)).astype(np.float32)
    full = full.reshape(freqs * 2 * loads, times * loads)
    high = full.astype(jnp.bfloat16)
    rest = (full - high.astype(np.float32)).astype(jnp.bfloat16)
    return np.concatenate([high, rest], axis=1)


def dot(left, right):
    return jnp.dot(left, right, preferred_element_type=jnp.float32)


def kernel(
    n_freq, n_unk, chunk,
    ts_hbm, w_hbm, o_hbm, c_hbm, f_hbm, out_ref,
    ts, w, o, c, f, near, far, mixed, o_even, c_even, f_even,
    sp, rb_even, rb_odd, xs, xin, acc,
    load_sem, send_sem, recv_sem, share_send, share_recv, pass_send, pass_recv,
    hop_send, hop_recv, hand_send, hand_recv, ready,
):
    me = lax.axis_index("freq")
    pos = lax.axis_index("unk")
    loads = ts.shape[1]
    rows = o.shape[1]
    slot_rows = 2 * loads
    n_far = max(1, n_freq // 4)
    n_near = n_freq - n_far
    is_odd = lax.rem(pos, 2) == 1
    is_even = jnp.logical_not(is_odd)
    partner = pos + 1 - 2 * lax.rem(pos, 2)
    first_pair = pos < 2
    later_pair = pos >= 2
    has_next = pos + 2 < n_unk
    near_slots, far_slots = pl.ds(0, n_near), pl.ds(n_near, n_far)
    groups = (near_slots, far_slots)

    def upper(freq):
        return (freq * 2) // n_freq

    def slot_of(source, target):
        return lax.rem(source + n_freq - n_far * upper(target), n_freq)

    def remote(src, dst, send, recv, unk, freq=me):
        return pltpu.make_async_remote_copy(
            src_ref=src, dst_ref=dst, send_sem=send, recv_sem=recv,
            device_id={"freq": freq, "unk": unk}, device_id_type=MESH,
        )

    loaded = [
        pltpu.make_async_copy(src, dst, load_sem.at[i])
        for i, (src, dst) in enumerate(
            [(ts_hbm, ts), (w_hbm, w), (o_hbm.at[:, 0], o), (c_hbm.at[:, 0], c), (f_hbm.at[:, 0], f)]
        )
    ]
    loaded[0].start()
    loaded[1].start()

    barrier = pltpu.get_barrier_semaphore()

    def greet(freq, unk):
        pl.semaphore_signal(
            barrier, inc=1, device_id={"freq": freq, "unk": unk}, device_id_type=MESH
        )

    def other(d):
        rising = (d - 1) + (d - 1 >= me).astype(jnp.int32)
        falling = (n_freq - d) - (n_freq - d <= me).astype(jnp.int32)
        return upper(me) * rising + (1 - upper(me)) * falling

    @pl.when(is_odd)
    def _():
        for d in range(1, n_freq):
            greet(other(d), pos)

        @pl.when(later_pair)
        def _():
            greet(me, pos - 2)

    greet(me, partner)
    loaded[2].start()

    @pl.when(pos >= 1)
    def _():
        loaded[3].start()

    @pl.when(later_pair)
    def _():
        loaded[4].start()

    def share(i):
        src = (o_hbm, c_hbm, f_hbm)[i]
        dst = (o_even, c_even, f_even)[i]
        return remote(src.at[:, 0], dst, share_send.at[i], share_recv.at[i], partner)

    @pl.when(is_even)
    def _():
        pl.semaphore_wait(barrier, 1)
        share(0).start()

    loaded[0].wait()
    loaded[1].wait()
    samples = ts[...].astype(jnp.float32).reshape(-1, rows).astype(jnp.bfloat16)
    spectra = dot(w[...], jnp.concatenate([samples, samples], axis=0))
    sp[...] = spectra.reshape(sp.shape).astype(jnp.bfloat16)

    def spread(kind, target):
        slot = slot_of(me, target)
        group = (slot >= n_near).astype(jnp.int32)
        return remote(
            sp.at[target], (rb_even, rb_odd)[kind].at[slot],
            send_sem.at[0], recv_sem.at[2 * kind + group], pos + 1 - kind, target,
        )

    def product(base, left, weights, dst):
        def part(i):
            at = pl.ds(pl.multiple_of(i * chunk, chunk), chunk)
            real, imag = left[0, at, :], left[1, at, :]
            both = weights[...].reshape(2 * rows, rows)
            new_real = dot(jnp.concatenate([real, -imag], axis=1), both)
            dst[0, at, :] = (base[0, at, :].astype(jnp.float32) + new_real).astype(jnp.bfloat16)
            new_imag = dot(jnp.concatenate([imag, real], axis=1), both)
            dst[1, at, :] = (base[1, at, :].astype(jnp.float32) + new_imag).astype(jnp.bfloat16)

        pl.loop(0, rows // chunk)(part)

    def times(x, weights):
        direct = dot(x, weights[0])
        turned = dot(x, weights[1]).reshape(-1, slot_rows, rows)
        turned = jnp.concatenate([-turned[:, loads:], turned[:, :loads]], axis=1)
        return direct + turned.reshape(-1, rows)

    def flat(value):
        wide = value.astype(jnp.float32).reshape(-1, rows)
        return wide, wide.astype(jnp.bfloat16)

    def slots(value):
        return value.reshape(-1, slot_rows, rows)

    def emit(value):
        value = slots(value)

        def put(ordered):
            for part in range(2):
                at = slice(part * loads, (part + 1) * loads)
                out_ref[part, 0] = ordered[:, at].reshape(-1, rows).astype(jnp.bfloat16)

        @pl.when(upper(me) == 0)
        def _():
            put(value)

        @pl.when(upper(me) == 1)
        def _():
            put(jnp.concatenate([value[n_near:], value[:n_near]], axis=0))

    def pass_on(i):
        at = groups[i]
        return remote(rb_even.at[at], rb_even.at[at], pass_send.at[i], pass_recv.at[i], partner)

    def hop(i):
        at = groups[i]
        return remote(xs.at[:, at], xin.at[:, at], hop_send.at[i], hop_recv.at[i], lax.rem(pos + 2, n_unk))

    def hand_on(i):
        at = groups[i]
        return remote(xin.at[:, at], xin.at[:, at], hand_send.at[i], hand_recv.at[i], partner)

    def received(kind, group):
        count = n_far if group else n_near - kind
        at = pl.ds(n_near if group else 0, count)
        ref = (rb_even, rb_odd)[kind].at[at]
        remote(ref, ref, send_sem.at[0], recv_sem.at[2 * kind + group], partner).wait_recv()

    @pl.when(is_odd)
    def _():
        pl.semaphore_wait(barrier, n_freq + has_next.astype(jnp.int32))
        pl.semaphore_signal(
            ready, inc=1, device_id={"freq": me, "unk": partner}, device_id_type=MESH
        )
        for d in range(1, n_freq):
            spread(1, other(d)).start()
        rb_odd[slot_of(me, me)] = sp[me]

        loaded[2].wait()
        loaded[3].wait()
        product(c, c, o, near)

        @pl.when(later_pair)
        def _():
            loaded[4].wait()
            product(f, f, o, far)

        share(0).wait_recv()
        product(near, o_even, near, mixed)

        @pl.when(first_pair)
        def _():
            for i, (low, high) in enumerate([(0, n_near), (n_near, n_freq)]):
                received(1, i)
                wide, tight = flat(rb_odd[low:high])
                driven = wide + times(tight, o)
                received(0, i)
                pass_on(i).start()
                wide, tight = flat(rb_even[low:high])
                xs[0, low:high] = slots(wide + times(tight, o_even)).astype(jnp.bfloat16)
                solved = slots(driven - times(tight, mixed))
                xs[1, low:high] = solved.astype(jnp.bfloat16)
                acc[low:high] = solved

                @pl.when(has_next)
                def _():
                    hop(i).start()

            emit(acc[...])

        @pl.when(later_pair)
        def _():
            for i in range(2):
                received(1, i)
                received(0, i)
                pass_on(i).start()
            wide, tight = flat(rb_odd[...])
            acc[...] = slots(wide + times(tight, o))
            share(1).wait_recv()
            share(2).wait_recv()
            for i in range(2):
                hop(i).wait_recv()
                hand_on(i).start()
            before = flat(xin[0])[1]
            last = flat(xin[1])[1]
            rest = flat(rb_even[...])[0] - times(last, c_even) - times(before, f_even)
            tight = rest.astype(jnp.bfloat16)
            solved = acc[...].reshape(-1, rows) - times(last, far) - times(tight, mixed)
            if n_unk > 4:
                @pl.when(has_next)
                def _():
                    xs[0] = slots(rest + times(tight, o_even)).astype(jnp.bfloat16)
                    xs[1] = slots(solved).astype(jnp.bfloat16)
                    hop(0).start()
                    hop(1).start()
            emit(solved)
            for i in range(2):
                hand_on(i).wait_send()

        for i in range(2):
            pass_on(i).wait_send()
        sent = sp.at[pl.ds(0, n_freq - 1)]
        remote(sent, sent, send_sem.at[0], recv_sem.at[0], partner).wait_send()

        @pl.when(has_next)
        def _():
            for i in range(2):
                hop(i).wait_send()

    @pl.when(is_even)
    def _():
        pl.semaphore_wait(ready, 1)
        for d in range(1, n_freq):
            spread(0, other(d)).start()
        spread(0, me).start()

        @pl.when(later_pair)
        def _():
            share(1).start()
            share(2).start()

        loaded[2].wait()

        @pl.when(later_pair)
        def _():
            loaded[3].wait()
            product(c, c, o, near)
            loaded[4].wait()
            product(f, f, o, far)

        for i in range(2):
            pass_on(i).wait_recv()
        wide, tight = flat(rb_even[...])
        acc[...] = slots(wide + times(tight, o))

        @pl.when(later_pair)
        def _():
            for i in range(2):
                hand_on(i).wait_recv()
            acc[...] -= slots(times(flat(xin[1])[1], near) + times(flat(xin[0])[1], far))

        emit(acc[...])
        share(0).wait_send()

        @pl.when(later_pair)
        def _():
            share(1).wait_send()
            share(2).wait_send()

        remote(sp, sp, send_sem.at[0], recv_sem.at[0], partner).wait_send()


def per_device(n_freq, n_unk, time_samples, inverse_offset, coupling_near, coupling_far):
    times, loads, rows = time_samples.shape
    freqs = inverse_offset.shape[1] * n_freq
    table = jnp.asarray(transform_matrix(times, freqs, loads))
    bf16 = jnp.bfloat16
    block = pltpu.VMEM((2, rows, rows), bf16)
    wide = (n_freq, 2 * loads, rows)
    dma = pltpu.SemaphoreType.DMA
    return pl.pallas_call(
        functools.partial(kernel, n_freq, n_unk, min(256, rows)),
        out_shape=pltpu.VMEM((2, 1, n_freq * loads, rows), bf16),
        in_specs=[pl.BlockSpec(memory_space=pl.ANY)] * 5,
        out_specs=pl.BlockSpec(memory_space=pltpu.VMEM),
        scratch_shapes=[
            pltpu.VMEM(time_samples.shape, bf16),
            pltpu.VMEM(table.shape, bf16),
            *[block] * 9,
            pltpu.VMEM(wide, bf16),
            pltpu.VMEM(wide, bf16),
            pltpu.VMEM(wide, bf16),
            pltpu.VMEM((2, *wide), bf16),
            pltpu.VMEM((2, *wide), bf16),
            pltpu.VMEM(wide, jnp.float32),
            dma((5,)), dma((1,)), dma((4,)), dma((3,)), dma((3,)),
            dma((2,)), dma((2,)), dma((2,)), dma((2,)), dma((2,)), dma((2,)),
            pltpu.SemaphoreType.REGULAR,
        ],
        compiler_params=pltpu.CompilerParams(collective_id=0, has_side_effects=True),
    )(time_samples, table, inverse_offset, coupling_near, coupling_far)


def solution(mesh):
    placed = (
        P(None, "freq", "unk"),
        P(None, "freq", "unk", None),
        P(None, "freq", "unk", None),
        P(None, "freq", "unk", None),
    )
    return jax.shard_map(
        functools.partial(per_device, mesh.shape["freq"], mesh.shape["unk"]),
        mesh=mesh,
        in_specs=placed,
        out_specs=P(None, "freq", None, "unk"),
        check_vma=False,
    )
```

```python
import functools
import math

import jax
import jax.numpy as jnp
import numpy as np
from jax import lax
from jax.experimental import pallas as pl
from jax.experimental.pallas import tpu as pltpu
from jax.sharding import PartitionSpec as P

MESH = pl.DeviceIdType.MESH


def transform_matrix(times, freqs, loads):
    moment = np.arange(times)
    angle = (np.arange(freqs)[:, None] * moment[None, :] % times) * (2.0 * math.pi / times)
    damping = np.power(0.5, moment / times) / math.sqrt(times)
    table = np.stack([damping * np.cos(angle), -damping * np.sin(angle)], axis=1)
    full = np.einsum("kct,lm->kcltm", table, np.eye(loads)).astype(np.float32)
    full = full.reshape(freqs * 2 * loads, times * loads)
    high = full.astype(jnp.bfloat16)
    rest = (full - high.astype(np.float32)).astype(jnp.bfloat16)
    return np.concatenate([high, rest], axis=1)


def dot(left, right):
    return jnp.dot(left, right, preferred_element_type=jnp.float32)


def kernel(
    n_freq, n_unk, n_far, chunk,
    ts_hbm, w_hbm, o_hbm, c_hbm, f_hbm, out_ref,
    ts, w, o, c, f, near, far, mixed, o_even, c_even, f_even,
    sp, rb_even, rb_odd, xs, xs_far, xin, xin_far, acc, tail,
    load_sem, send_sem, recv_sem, share_send, share_recv, pass_send, pass_recv,
    hop_send, hop_recv, hand_send, hand_recv, ready,
):
    me = lax.axis_index("freq")
    pos = lax.axis_index("unk")
    loads = ts.shape[1]
    rows = o.shape[1]
    n_near = n_freq - n_far
    is_odd = lax.rem(pos, 2) == 1
    is_even = jnp.logical_not(is_odd)
    partner = pos + 1 - 2 * lax.rem(pos, 2)
    first_pair = pos < 2
    later_pair = pos >= 2
    has_next = pos + 2 < n_unk
    quarter = (me * 4) // n_freq
    bounds = ((0, n_near), (n_near, n_freq))
    x_out, x_in, kept = (xs, xs_far), (xin, xin_far), (acc, tail)

    def upper(freq):
        return (freq * 2) // n_freq

    def slot_of(source, target):
        return lax.rem(source + n_freq - n_far * upper(target), n_freq)

    def remote(src, dst, send, recv, unk, freq=me):
        return pltpu.make_async_remote_copy(
            src_ref=src, dst_ref=dst, send_sem=send, recv_sem=recv,
            device_id={"freq": freq, "unk": unk}, device_id_type=MESH,
        )

    loaded = [
        pltpu.make_async_copy(src, dst, load_sem.at[i])
        for i, (src, dst) in enumerate(
            [(ts_hbm, ts), (w_hbm, w), (o_hbm.at[:, 0], o), (c_hbm.at[:, 0], c), (f_hbm.at[:, 0], f)]
        )
    ]
    loaded[0].start()
    loaded[1].start()

    barrier = pltpu.get_barrier_semaphore()

    def greet(freq, unk):
        pl.semaphore_signal(
            barrier, inc=1, device_id={"freq": freq, "unk": unk}, device_id_type=MESH
        )

    def other(d):
        rising = (d - 1) + (d - 1 >= me).astype(jnp.int32)
        falling = (n_freq - d) - (n_freq - d <= me).astype(jnp.int32)
        return upper(me) * rising + (1 - upper(me)) * falling

    @pl.when(is_odd)
    def _():
        for d in range(1, n_freq):
            greet(other(d), pos)

        @pl.when(later_pair)
        def _():
            greet(me, pos - 2)

    greet(me, partner)
    loaded[2].start()

    @pl.when(pos >= 1)
    def _():
        loaded[3].start()

    @pl.when(later_pair)
    def _():
        loaded[4].start()

    def share(i):
        src = (o_hbm, c_hbm, f_hbm)[i]
        dst = (o_even, c_even, f_even)[i]
        return remote(src.at[:, 0], dst, share_send.at[i], share_recv.at[i], partner)

    @pl.when(is_even)
    def _():
        @pl.when(later_pair)
        def _():
            greet(me, pos - 1)

        pl.semaphore_wait(barrier, 1)
        share(0).start()

        @pl.when(later_pair)
        def _():
            share(1).start()
            share(2).start()

    loaded[0].wait()
    loaded[1].wait()
    samples = ts[...].astype(jnp.float32).reshape(-1, rows).astype(jnp.bfloat16)
    spectra = dot(w[...], jnp.concatenate([samples, samples], axis=0))
    sp[...] = spectra.reshape(sp.shape).astype(jnp.bfloat16)

    def spread(kind, target):
        slot = slot_of(me, target)
        group = (slot >= n_near).astype(jnp.int32)
        return remote(
            sp.at[target], (rb_even, rb_odd)[kind].at[slot],
            send_sem.at[0], recv_sem.at[2 * kind + group], pos + 1 - kind, target,
        )

    def product(base, left, weights, dst):
        def part(i):
            at = pl.ds(pl.multiple_of(i * chunk, chunk), chunk)
            real, imag = left[0, at, :], left[1, at, :]
            both = weights[...].reshape(2 * rows, rows)
            new_real = dot(jnp.concatenate([real, -imag], axis=1), both)
            dst[0, at, :] = (base[0, at, :].astype(jnp.float32) + new_real).astype(jnp.bfloat16)
            new_imag = dot(jnp.concatenate([imag, real], axis=1), both)
            dst[1, at, :] = (base[1, at, :].astype(jnp.float32) + new_imag).astype(jnp.bfloat16)

        pl.loop(0, rows // chunk)(part)

    def near_product():
        loaded[2].wait()
        loaded[3].wait()
        product(c, c, o, near)

    def far_product():
        loaded[4].wait()
        product(f, f, o, far)

    def mixed_product():
        share(0).wait_recv()
        product(near, o_even, near, mixed)

    def times(x, weights):
        direct = dot(x, weights[0])
        turned = dot(x, weights[1])
        half = x.shape[0] // 2
        return direct + jnp.concatenate([-turned[half:], turned[:half]], axis=0)

    def ordered(ref, group):
        low, high = bounds[group]
        value = ref[low:high].astype(jnp.float32)
        value = jnp.concatenate(
            [value[:, :loads].reshape(-1, rows), value[:, loads:].reshape(-1, rows)], axis=0
        )
        return value, value.astype(jnp.bfloat16)

    def emit(close, distant):
        swapped = upper(me) == 1
        for part in range(2):
            a = close[part * n_near * loads:(part + 1) * n_near * loads]
            b = distant[part * n_far * loads:(part + 1) * n_far * loads]
            value = jnp.where(
                swapped, jnp.concatenate([b, a], axis=0), jnp.concatenate([a, b], axis=0)
            )
            out_ref[part, 0] = value.astype(jnp.bfloat16)

    def pass_on(i):
        at = pl.ds(bounds[i][0], bounds[i][1] - bounds[i][0])
        return remote(rb_even.at[at], rb_even.at[at], pass_send.at[i], pass_recv.at[i], partner)

    def hop(i):
        return remote(x_out[i], x_in[i], hop_send.at[i], hop_recv.at[i], lax.rem(pos + 2, n_unk))

    def hop_even():
        return remote(xs_far, xin_far, hop_send.at[2], hop_recv.at[2], lax.rem(pos + 1, n_unk))

    def hand_on():
        return remote(xin, xin, hand_send.at[0], hand_recv.at[0], partner)

    def received(kind, group):
        count = n_far if group else n_near - kind
        at = pl.ds(n_near if group else 0, count)
        ref = (rb_even, rb_odd)[kind].at[at]
        remote(ref, ref, send_sem.at[0], recv_sem.at[2 * kind + group], partner).wait_recv()

    @pl.when(is_odd)
    def _():
        @pl.when(quarter < 2)
        def _():
            near_product()

        @pl.when(quarter == 0)
        def _():
            @pl.when(first_pair)
            def _():
                mixed_product()

            @pl.when(later_pair)
            def _():
                far_product()

        pl.semaphore_wait(barrier, n_freq + 2 * has_next.astype(jnp.int32))
        pl.semaphore_signal(
            ready, inc=1, device_id={"freq": me, "unk": partner}, device_id_type=MESH
        )
        for d in range(1, n_freq):
            spread(1, other(d)).start()
        rb_odd[slot_of(me, me)] = sp[me]

        @pl.when(quarter >= 2)
        def _():
            near_product()

        @pl.when(jnp.logical_and(quarter >= 1, later_pair))
        def _():
            far_product()

        @pl.when(jnp.logical_or(quarter >= 1, later_pair))
        def _():
            mixed_product()

        @pl.when(first_pair)
        def _():
            for i in range(2):
                received(1, i)
                wide, tight = ordered(rb_odd, i)
                driven = wide + times(tight, o)
                received(0, i)
                pass_on(i).start()
                wide, tight = ordered(rb_even, i)
                x_out[i][0] = (wide + times(tight, o_even)).astype(jnp.bfloat16)
                solved = driven - times(tight, mixed)
                x_out[i][1] = solved.astype(jnp.bfloat16)
                kept[i][...] = solved

                @pl.when(has_next)
                def _():
                    hop(i).start()
                    if i == 1:
                        hop_even().start()

            emit(acc[...], tail[...])

        @pl.when(later_pair)
        def _():
            for i in range(2):
                received(1, i)
                received(0, i)
                pass_on(i).start()
            for i in range(2):
                wide, tight = ordered(rb_odd, i)
                kept[i][...] = wide + times(tight, o)
            share(1).wait_recv()
            share(2).wait_recv()
            done = []
            for i in range(2):
                rest = ordered(rb_even, i)[0]
                hop(i).wait_recv()
                if i == 0:
                    hand_on().start()
                rest = rest - times(x_in[i][1], c_even) - times(x_in[i][0], f_even)
                tight = rest.astype(jnp.bfloat16)
                solved = kept[i][...] - times(x_in[i][1], far) - times(tight, mixed)
                if n_unk > 4:
                    @pl.when(has_next)
                    def _():
                        x_out[i][0] = (rest + times(tight, o_even)).astype(jnp.bfloat16)
                        x_out[i][1] = solved.astype(jnp.bfloat16)
                        hop(i).start()
                        if i == 1:
                            hop_even().start()
                if i == 0:
                    acc[...] = solved
            emit(acc[...], solved)
            hand_on().wait_send()

        for i in range(2):
            pass_on(i).wait_send()
        sent = sp.at[pl.ds(0, n_freq - 1)]
        remote(sent, sent, send_sem.at[0], recv_sem.at[0], partner).wait_send()

        @pl.when(has_next)
        def _():
            for i in range(2):
                hop(i).wait_send()
            hop_even().wait_send()

    @pl.when(is_even)
    def _():
        @pl.when(jnp.logical_and(quarter < 2, later_pair))
        def _():
            near_product()

        @pl.when(jnp.logical_and(quarter == 0, later_pair))
        def _():
            far_product()

        pl.semaphore_wait(ready, 1)
        for d in range(1, n_freq):
            spread(0, other(d)).start()
        spread(0, me).start()

        @pl.when(jnp.logical_and(quarter >= 2, later_pair))
        def _():
            near_product()

        @pl.when(jnp.logical_and(quarter >= 1, later_pair))
        def _():
            far_product()

        @pl.when(first_pair)
        def _():
            loaded[2].wait()

        for i in range(2):
            pass_on(i).wait_recv()
            wide, tight = ordered(rb_even, i)
            kept[i][...] = wide + times(tight, o)

        @pl.when(later_pair)
        def _():
            for i in range(2):
                if i == 0:
                    hand_on().wait_recv()
                else:
                    hop_even().wait_recv()
                kept[i][...] -= times(x_in[i][1], near) + times(x_in[i][0], far)

        emit(acc[...], tail[...])
        share(0).wait_send()

        @pl.when(later_pair)
        def _():
            share(1).wait_send()
            share(2).wait_send()

        remote(sp, sp, send_sem.at[0], recv_sem.at[0], partner).wait_send()


def per_device(n_freq, n_unk, time_samples, inverse_offset, coupling_near, coupling_far):
    times, loads, rows = time_samples.shape
    freqs = inverse_offset.shape[1] * n_freq
    table = jnp.asarray(transform_matrix(times, freqs, loads))
    bf16 = jnp.bfloat16
    n_far = max(1, n_freq // 4)
    rows_near, rows_far = 2 * (n_freq - n_far) * loads, 2 * n_far * loads
    block = pltpu.VMEM((2, rows, rows), bf16)
    wide = pltpu.VMEM((n_freq, 2 * loads, rows), bf16)
    dma = pltpu.SemaphoreType.DMA
    return pl.pallas_call(
        functools.partial(kernel, n_freq, n_unk, n_far, min(256, rows)),
        out_shape=pltpu.VMEM((2, 1, n_freq * loads, rows), bf16),
        in_specs=[pl.BlockSpec(memory_space=pl.ANY)] * 5,
        out_specs=pl.BlockSpec(memory_space=pltpu.VMEM),
        scratch_shapes=[
            pltpu.VMEM(time_samples.shape, bf16),
            pltpu.VMEM(table.shape, bf16),
            *[block] * 9,
            *[wide] * 3,
            *[pltpu.VMEM((2, rows_near, rows), bf16), pltpu.VMEM((2, rows_far, rows), bf16)] * 2,
            pltpu.VMEM((rows_near, rows), jnp.float32),
            pltpu.VMEM((rows_far, rows), jnp.float32),
            dma((5,)), dma((1,)), dma((4,)), dma((3,)), dma((3,)),
            dma((2,)), dma((2,)), dma((3,)), dma((3,)), dma((1,)), dma((1,)),
            pltpu.SemaphoreType.REGULAR,
        ],
        compiler_params=pltpu.CompilerParams(collective_id=0, has_side_effects=True),
    )(time_samples, table, inverse_offset, coupling_near, coupling_far)


def solution(mesh):
    placed = (
        P(None, "freq", "unk"),
        P(None, "freq", "unk", None),
        P(None, "freq", "unk", None),
        P(None, "freq", "unk", None),
    )
    return jax.shard_map(
        functools.partial(per_device, mesh.shape["freq"], mesh.shape["unk"]),
        mesh=mesh,
        in_specs=placed,
        out_specs=P(None, "freq", None, "unk"),
        check_vma=False,
    )
```
